32 devices in a mesh: tile: 4 (over x, core), blk: 8 (over z, y).
Axes of the slice: x: 2, y: 2, z: 4, core: 2. Of those that a mesh axis runs over, the one named last changes fastest.
Arguments:
- tokens: bfloat16 [32768, 384], P(('tile', 'blk')), may hold values from -52 to 52
- ln_gain: float32 [384], replicated, may hold values from 0.1 to 1.9
- route: int32 [32768, 2], P(('tile', 'blk')), may hold values from 0 to 15, all different within a row; in each aligned block of 1024 rows (0 to 1023, 1024 to 2047, ...) at most 192 rows name the same one
- gates: float32 [32768, 2], P(('tile', 'blk')), may hold values from 0.1 to 1
- w_gate: bfloat16 [16, 384, 1024], P('tile', 'blk'), may hold values from -0.3125 to 0.3125
- w_up: bfloat16 [16, 384, 1024], P('tile', 'blk'), may hold values from -0.3125 to 0.3125
- w_down: bfloat16 [16, 1024, 384], P('tile', 'blk'), may hold values from -0.1875 to 0.1875
- d_mixed: bfloat16 [32768, 384], P(('tile', 'blk')), may hold values from -6 to 6
Outputs:
- mixed: bfloat16 [32768, 384], P(('tile', 'blk'))
- grad_gates: float32 [32768, 2], P(('tile', 'blk'))
- grad_tokens: bfloat16 [32768, 384], P(('tile', 'blk'))
- grad_w_gate: float32 [16, 384, 1024], P('tile', 'blk')
- grad_w_up: float32 [16, 384, 1024], P('tile', 'blk')
- grad_w_down: float32 [16, 1024, 384], P('tile', 'blk')
The draws below stay inside these ranges and needn't reach their ends.
Inputs may be any that keep to these rules, and one draw needn't show every extreme that they name: `route`: each row names 2 different experts; within the rows of one device no expert is named more than 192 times, a bound that some block reaches.
All inputs are finite; a program needn't handle non-finite values.
Results may differ from the reference program's by a relative error of at most 0.014.
Values may be sent and summed in bfloat16 or wider, within the bound.
A program may use at most 192 MiB of HBM per device.

```python
import math
import jax
import jax.numpy as jnp
import numpy as np
from jax import lax

D = 384
HID = 1024
TOPK = 2
TOK_DEV = 1024
EXPERTS = 16
CAP = 192
TOKENS = 32768
N_TILE = 4
N_BLK = 8


def draw_tokens(key, part):
    key_cols, key_rows, key_offs, key_base = jax.random.split(key, 4)
    col_scale = jnp.exp(jax.random.uniform(key_cols, (D,), jnp.float32, 0.0, math.log(10.0)))
    row_scale = jnp.exp(jax.random.uniform(key_rows, (TOKENS, 1), jnp.float32, 0.0, math.log(10.0)))
    offsets = jnp.clip(jax.random.normal(key_offs, (D,), jnp.float32), -3.0, 3.0) * 0.5
    base_draw = jnp.clip(jax.random.normal(key_base, (TOKENS, D), jnp.float32), -5.0, 5.0)
    return ((base_draw * col_scale + offsets) * row_scale * 0.1).astype(jnp.bfloat16)


def steps_of(own_key, extent, cuts, least, top_value):
    def one(dim, parts):
        steps = jax.random.uniform(jax.random.fold_in(jax.random.fold_in(own_key, 6), dim), (parts,), jnp.float32, least / len(cuts), top_value / len(cuts))
        return jnp.repeat(jnp.exp(steps), extent[dim] // parts).reshape((-1,) + (1,) * (len(extent) - dim - 1))

    gain = one(*cuts[0])
    for cut in cuts[1:]:
        gain = gain * one(*cut)
    return gain


def routed_block(rng, own, number, rows, number_of, top, reach, skew):
    order = jax.random.permutation(rng, number_of)
    packed, usual = portions_of(number_of, rows * top, reach, skew, True), portions_of(number_of, rows * top, reach, skew, False)
    places = jnp.arange(number_of)

    def named(lengths, rotation):
        used = int((lengths > 0).sum())
        fixed = max(1, used // 4)
        moved = fixed + (places - fixed + rotation * (used - fixed)) % max(1, number_of - fixed)
        return jnp.zeros((number_of,), jnp.int32).at[order[jnp.where(places < fixed, places, moved)]].set(jnp.asarray(lengths, jnp.int32))

    lengths = jnp.where(number % 4 == 0, named(packed, number // 4), named(usual, number - number // 4 - 1))
    mixed = jax.random.permutation(jax.random.fold_in(own, 3), number_of)
    giver, receiver = mixed[0:number_of // 2 * 2:2], mixed[1:number_of // 2 * 2:2]
    margin = jnp.minimum(lengths[giver] - 1, reach - lengths[receiver]) // 2
    margin = jnp.where((giver == order[0]) | (receiver == order[0]) | (lengths[receiver] == 0), 0, jnp.maximum(margin, 0))
    moved = jax.random.randint(jax.random.fold_in(own, 4), (number_of // 2,), 0, 1 << 20) % (margin + 1)
    lengths = lengths.at[giver].add(-moved).at[receiver].add(moved)
    members = jnp.searchsorted(jnp.cumsum(lengths), jnp.arange(rows * top), side="right").astype(jnp.int32)
    listing = members.reshape(top, rows).T
    listing = listing[jax.random.permutation(jax.random.fold_in(own, 1), rows)]
    rotation = jax.random.randint(jax.random.fold_in(own, 2), (rows, 1), 0, top)
    return jnp.take_along_axis(listing, (jnp.arange(top)[None, :] + rotation) % top, axis=1)


def portions_of(count, total, limit, skew, full):
    loads = [(1 << 20) // math.isqrt(rank ** skew) + 1 for rank in range(1, count + 1)]
    largest = limit if full else min(limit, max(-(-total // count), total * loads[0] // sum(loads)))
    least = 1 if total - largest >= count - 1 else 0
    given, surplus = [largest] + [least] * (count - 1), total - largest - least * (count - 1)
    while surplus > 0:
        free = [i for i in range(1, count) if given[i] < largest] or [i for i in range(1, count) if given[i] < limit]
        whole, left = sum([loads[i] for i in free]), surplus
        for i in free:
            more = min(limit - given[i], max(1, left * loads[i] // whole), surplus)
            given[i] = given[i] + more
            surplus = surplus - more
    return np.array(given)


def noise(key, shape, scale, reach, cuts=(), held_as=jnp.bfloat16):
    values = scale * jax.random.normal(key, shape, jnp.float32)
    if cuts:
        values = values * steps_of(key, shape, cuts, -0.22, 0.18)
    return jnp.clip(values, -reach, reach).astype(held_as)


def setup_inputs(seed: int = 0) -> dict:
    streams_of = jax.random.split(jax.random.key(seed), 9)
    tokens = draw_tokens(jax.random.fold_in(streams_of[8], 71), 0)
    ln_gain = jnp.clip(1.0 + 0.18 * jax.random.normal(streams_of[1], (D,), jnp.float32), 0.1, 1.9)
    route_keys = jax.random.split(jax.random.fold_in(streams_of[2], 1), TOKENS // TOK_DEV)
    route_turns = jax.random.permutation(jax.random.fold_in(streams_of[2], 3), TOKENS // TOK_DEV)
    route = jax.vmap(lambda own, number: routed_block(jax.random.fold_in(streams_of[2], 2), own, number, TOK_DEV, EXPERTS, TOPK, CAP, 2))(route_keys, route_turns).reshape((TOKENS, TOPK))
    gates = jnp.clip(jnp.exp(math.log(1.0) - 2.3025851 * jax.random.uniform(streams_of[3], (TOKENS, TOPK), jnp.float32) ** steps_of(streams_of[3], (TOKENS, TOPK), ((0, 32),), -0.2, 0.2)), 0.1, 1.0)
    w_gate = noise(streams_of[4], (EXPERTS, D, HID), D ** -0.5, 0.3125, ((0, 4), (1, 8)))
    w_up = noise(streams_of[5], (EXPERTS, D, HID), D ** -0.5, 0.3125, ((0, 4), (1, 8)))
    w_down = noise(streams_of[6], (EXPERTS, HID, D), HID ** -0.5, 0.1875, ((0, 4), (1, 8)))
    d_mixed = noise(streams_of[7], (TOKENS, D), 1.0, 6.0, ((0, 32),))
    return dict(tokens=tokens, ln_gain=ln_gain, route=route, gates=gates, w_gate=w_gate, w_up=w_up, w_down=w_down, d_mixed=d_mixed)


def layer_norm(values, ln_gain):
    centre = lax.optimization_barrier(jnp.mean(values, axis=-1, keepdims=True))
    centred = values - centre
    spread = lax.optimization_barrier(jnp.mean(centred * centred, axis=-1, keepdims=True))
    return values * lax.rsqrt(spread + 1e-05) * ln_gain

def reference(tokens, ln_gain, route, gates, w_gate, w_up, w_down, d_mixed):
    tokens_wide = tokens.astype(jnp.float32)
    normed = layer_norm(tokens_wide, ln_gain).astype(jnp.bfloat16)
    count = TOKENS * TOPK
    most_rows = N_TILE * N_BLK * CAP
    flat_route = route.reshape(-1).astype(jnp.int32)
    owner_token = jnp.arange(count, dtype=jnp.int32) // TOPK
    onehot = (flat_route[:, None] == jnp.arange(EXPERTS, dtype=jnp.int32)[None, :]).astype(jnp.int32)
    slot_rank = lax.optimization_barrier(jnp.sum((jnp.cumsum(onehot, axis=0) - 1) * onehot, axis=1)).astype(jnp.int32)
    slot_index = (flat_route * most_rows + slot_rank).astype(jnp.int32)
    table = jnp.full((EXPERTS * most_rows,), count, jnp.int32)
    table = table.at[slot_index].set(jnp.arange(count, dtype=jnp.int32)).reshape(EXPERTS, most_rows)
    d_wide = d_mixed.astype(jnp.float32)
    d_assign = (gates.reshape(-1)[:, None] * d_wide[owner_token]).astype(jnp.bfloat16)
    normed_pad = jnp.concatenate([normed, jnp.zeros((1, D), jnp.bfloat16)], axis=0)
    d_pad = jnp.concatenate([d_assign, jnp.zeros((1, D), jnp.bfloat16)], axis=0)
    token_pad = jnp.concatenate([owner_token, jnp.full((1,), TOKENS, jnp.int32)], axis=0)

    def per_expert(inputs):
        indices, weight_gate, weight_up, weight_down = inputs
        inputs_rows = normed_pad[token_pad[indices]]
        d_rows = d_pad[indices]
        gate_pre = jnp.dot(inputs_rows, weight_gate, preferred_element_type=jnp.float32)
        up_pre = jnp.dot(inputs_rows, weight_up, preferred_element_type=jnp.float32)
        sigma_gate = jax.nn.sigmoid(gate_pre)
        hidden_act = (gate_pre * sigma_gate * up_pre).astype(jnp.bfloat16)
        expert_rows = jnp.dot(hidden_act, weight_down, preferred_element_type=jnp.float32).astype(jnp.bfloat16)
        d_act = jnp.dot(d_rows, weight_down.T, preferred_element_type=jnp.float32)
        d_gate = (d_act * up_pre * sigma_gate * (1.0 + gate_pre * (1.0 - sigma_gate))).astype(jnp.bfloat16)
        d_up = (d_act * gate_pre * sigma_gate).astype(jnp.bfloat16)
        d_in = (jnp.dot(d_gate, weight_gate.T, preferred_element_type=jnp.float32) + jnp.dot(d_up, weight_up.T, preferred_element_type=jnp.float32)).astype(jnp.bfloat16)
        grad_gate = jnp.dot(inputs_rows.T, d_gate, preferred_element_type=jnp.float32)
        grad_up = jnp.dot(inputs_rows.T, d_up, preferred_element_type=jnp.float32)
        grad_down = jnp.dot(hidden_act.T, d_rows, preferred_element_type=jnp.float32)
        return (expert_rows, d_in, grad_gate, grad_up, grad_down)
    out_rows, din_rows, grad_w_gate, grad_w_up, grad_w_down = lax.map(per_expert, (table, w_gate, w_up, w_down))
    expert_out = out_rows.reshape(-1, D)[slot_index].astype(jnp.float32).reshape(TOKENS, TOPK, D)
    mixed = lax.optimization_barrier(jnp.sum(gates[:, :, None] * expert_out, axis=1)).astype(jnp.bfloat16)
    grad_gates = lax.optimization_barrier(jnp.sum(d_wide[:, None, :] * expert_out, axis=-1))
    d_normed = lax.optimization_barrier(jnp.sum(din_rows.reshape(-1, D)[slot_index].astype(jnp.float32).reshape(TOKENS, TOPK, D), axis=1))

    def normalize(values):
        return layer_norm(values, ln_gain)
    unused, pullback = jax.vjp(normalize, tokens_wide)
    grad_tokens = pullback(d_normed)[0].astype(jnp.bfloat16)
    return (mixed, grad_gates, grad_tokens, grad_w_gate, grad_w_up, grad_w_down)
```

```python
import functools
import math

import jax
import jax.numpy as jnp
from jax import lax
from jax.experimental import pallas as pl
from jax.experimental.pallas import tpu as pltpu
from jax.sharding import PartitionSpec as P

F32 = jnp.float32
BF16 = jnp.bfloat16
MESH = pl.DeviceIdType.MESH


def matmul(left, right, dims=((1,), (0,))):
    return lax.dot_general(left, right, (dims, ((), ())), preferred_element_type=F32)


def onehot(mask):
    return mask.astype(F32).astype(BF16)


def both(*conditions):
    total = conditions[0]
    for condition in conditions[1:]:
        total = jnp.logical_and(total, condition)
    return total


def kernel(
    tiles, inner, outer, per_dev, cap,
    tok, gain, route_t, gates_t, w_gate, w_up, w_down, dmix,
    mixed, grad_gates, grad_tok, out_gate, out_up, out_dn,
    wgu, wdn, xs, xr, yr, ggu, gdn, rgu, rdn, fgu, fdn, tgu, tdn, prep, tmp, acc, cols, slot_r,
    load_sem, sw_send, sw_recv, ag_send, ag_recv, rs_send, rs_recv, fs_send, fs_recv,
    go_send, go_recv, go_own, back_send, back_recv, back_own,
):
    rows, feats = tok.shape
    hid = w_gate.shape[2]
    blks = inner * outer
    thin, deep = feats // blks, hid // blks
    half = hid // 2
    group = tiles * inner
    wide = inner * cap
    many = tiles * wide
    t = lax.axis_index("tile")
    b = lax.axis_index("blk")
    r = b // inner
    y = lax.rem(b, inner)
    order = (0, 2, 1)

    def device(tile, row, col):
        return dict(device_id=(tile, row * inner + col), device_id_type=MESH)

    def shards(part, name):
        if part == 2:
            return (w_down.at[name],)
        span = slice(part * half, (part + 1) * half)
        return (w_gate.at[name, :, span], w_up.at[name, :, span])

    def places(part, e, blk):
        if part == 2:
            return (wdn.at[e, blk],)
        return (wgu.at[e, part, 0, blk], wgu.at[e, part, 1, blk])

    def loads(part, e):
        return [
            pltpu.make_async_copy(src, dst, load_sem.at[e, part, i])
            for i, (src, dst) in enumerate(zip(shards(part, y * per_dev + e), places(part, e, b)))
        ]

    def swaps(part, e, col, blk, mark):
        return [
            pltpu.make_async_remote_copy(
                src_ref=src, dst_ref=dst, send_sem=sw_send.at[e, part, col, i],
                recv_sem=sw_recv.at[e, part, mark, i], **device(t, r, col),
            )
            for i, (src, dst) in enumerate(zip(shards(part, col * per_dev + e), places(part, e, blk)))
        ]

    def other_columns(action):
        for col in range(inner):
            pl.when(col != y)(functools.partial(action, col))

    def swap_start(e):
        for part in order:
            def go(col):
                for copy in swaps(part, e, col, b, y):
                    copy.start()
            other_columns(go)

    def weight_rows(part, e, row):
        span = pl.ds(row * inner, inner)
        return wdn.at[e, span] if part == 2 else wgu.at[e, part, :, span]

    def ag_copy(part, e, way, s, row):
        ref = weight_rows(part, e, row)
        return pltpu.make_async_remote_copy(
            src_ref=ref, dst_ref=ref, send_sem=ag_send.at[e, part, way, s],
            recv_sem=ag_recv.at[e, part, way, s], **device(t, r - 1 if way else r + 1, y),
        )

    def ag_has(way, s):
        return both(r >= 1, r + s < outer) if way else both(r + 1 < outer, r - s >= 0)

    def ag_sent_row(way, s):
        return r + s if way else r - s

    def ag_own(part, e):
        for copy in loads(part, e):
            copy.wait()

        def land(col):
            for copy in swaps(part, e, col, r * inner + col, col):
                copy.wait_recv()
        other_columns(land)
        for way in range(2):
            @pl.when(ag_has(way, 0))
            def _():
                ag_copy(part, e, way, 0, r).start()

    def ag_event(part, e, s):
        for way in range(2):
            row = r + 1 + s if way else r - 1 - s

            @pl.when(row < outer if way else row >= 0)
            def _():
                ag_copy(part, e, way, s, row).wait_recv()
                if s + 1 < outer - 1:
                    @pl.when(r >= 1 if way else r + 1 < outer)
                    def _():
                        ag_copy(part, e, way, s + 1, row).start()

    def grad_rows(part, e, row):
        span = pl.ds(row * inner, inner)
        return gdn.at[e, span] if part == 2 else ggu.at[e, part, :, span]

    def landed(part, e, way, k):
        return rdn.at[e, way, k] if part == 2 else rgu.at[e, part, way, k]

    def rs_copy(part, e, way, k):
        return pltpu.make_async_remote_copy(
            src_ref=grad_rows(part, e, k if way else outer - 1 - k), dst_ref=landed(part, e, way, k),
            send_sem=rs_send.at[e, part, way, k], recv_sem=rs_recv.at[e, part, way, k],
            **device(t, r - 1 if way else r + 1, y),
        )

    def fs_copy(part, e, col, mark):
        if part == 2:
            src, dst = gdn.at[e, r * inner + col], fdn.at[e, mark]
        else:
            src, dst = ggu.at[e, part, :, r * inner + col], fgu.at[e, part, mark]
        return pltpu.make_async_remote_copy(
            src_ref=src, dst_ref=dst, send_sem=fs_send.at[e, part, col],
            recv_sem=fs_recv.at[e, part, mark], **device(t, r, col),
        )

    def put(part, name, value):
        if part == 2:
            out_dn[name] = value
        else:
            span = slice(part * half, (part + 1) * half)
            out_gate[name, :, span] = value[0]
            out_up[name, :, span] = value[1]

    def rs_start(part, e):
        for way in range(2):
            far = outer - 1 - r if way else r

            @pl.when(far == 0)
            def _():
                for k in range(outer - 1):
                    rs_copy(part, e, way, k).start()

    def rs_event(part, e, step):
        for way in range(2):
            far = outer - 1 - r if way else r

            @pl.when(both(far > 0, far <= step))
            def _():
                k = step - far
                own, new = grad_rows(part, e, k if way else outer - 1 - k), landed(part, e, way, k)
                rs_copy(part, e, way, k).wait_recv()
                own[...] = (own[...].astype(F32) + new[...].astype(F32)).astype(BF16)
                rs_copy(part, e, way, k).start()

    def rs_final(part, e):
        total = tdn if part == 2 else tgu
        total[...] = grad_rows(part, e, r)[...].astype(F32)
        for way in range(2):
            far = outer - 1 - r if way else r

            @pl.when(far > 0)
            def _():
                k = outer - 1 - far
                rs_copy(part, e, way, k).wait_recv()
                total[...] += landed(part, e, way, k)[...].astype(F32)

        for col in range(inner):
            value = total[col] if part == 2 else total[:, col]

            @pl.when(col == y)
            def _():
                put(part, col * per_dev + e, value)

            @pl.when(col != y)
            def _():
                if part == 2:
                    gdn[e, r * inner + col] = value.astype(BF16)
                else:
                    ggu[e, part, :, r * inner + col] = value.astype(BF16)
                fs_copy(part, e, col, y).start()

    def rs_take(part, e):
        def take(col):
            fs_copy(part, e, col, col).wait_recv()
            put(part, col * per_dev + e, (fdn[e, col] if part == 2 else fgu[e, part, col]).astype(F32))
        other_columns(take)

    def exchange(e, jt, action, backward, mark):
        tile = lax.rem(t + jt, tiles)
        from_tile = lax.rem(t - jt + tiles, tiles)
        for col in range(inner):
            if backward:
                src, dst = xr.at[e, tile, col], yr.at[e, t, y]
                landing = yr.at[e, from_tile, col]
                sems = back_send, back_recv, back_own
            else:
                src, dst = xs.at[e, jt, col], xr.at[e, t, y]
                landing = xr.at[e, from_tile, col]
                sems = go_send, go_recv, go_own

            def here():
                return pltpu.make_async_copy(src, dst, sems[2].at[e])

            def there():
                return pltpu.make_async_remote_copy(
                    src_ref=src, dst_ref=landing if mark else dst,
                    send_sem=sems[0].at[e, jt, col], recv_sem=sems[1].at[e, jt, col if mark else y],
                    **device(tile, r, col),
                )

            mine = both(jt == 0, col == y)
            pl.when(mine)(lambda: action(here(), True))
            pl.when(jnp.logical_not(mine))(lambda: action(there(), False))

    def begin(copy, local):
        copy.start()

    def arrive(copy, local):
        if local:
            copy.wait()
        else:
            copy.wait_recv()

    def leave(copy, local):
        if not local:
            copy.wait_send()

    def everywhere(e, action, backward, mark):
        def one(jt, carry):
            exchange(e, jt, action, backward, mark)
            return carry
        lax.fori_loop(0, tiles, one, 0)

    def service(i, *lists):
        for events in lists:
            for place, event in events:
                pl.when(i == place)(event)

    def spread(count, makers):
        return [(min(i, count - 1), maker) for i, maker in enumerate(makers)]

    for e in range(per_dev):
        for part in order:
            for copy in loads(part, e):
                copy.start()

    barrier = pltpu.get_barrier_semaphore()
    for jt in range(tiles):
        for col in range(inner):
            @pl.when(jnp.logical_or(jt > 0, col != y))
            def _():
                pl.semaphore_signal(barrier, inc=1, **device(lax.rem(t + jt, tiles), r, col))

    @pl.when(r > 0)
    def _():
        pl.semaphore_signal(barrier, inc=1, **device(t, r - 1, y))

    @pl.when(r + 1 < outer)
    def _():
        pl.semaphore_signal(barrier, inc=1, **device(t, r + 1, y))

    pl.semaphore_wait(
        barrier, group - 1 + jnp.where(r > 0, 1, 0) + jnp.where(r + 1 < outer, 1, 0)
    )
    swap_start(0)

    block = min(256, rows)
    blocks = rows // block

    def slots(i, carry):
        base = pl.multiple_of(i * block, block)
        span = pl.ds(base, block)
        experts = group * per_dev
        names = lax.broadcasted_iota(jnp.int32, (experts, rows), 0)
        count = (route_t[0:1, :] == names).astype(F32) + (route_t[1:2, :] == names).astype(F32)
        row = lax.broadcasted_iota(jnp.int32, (rows, block), 0)
        col = lax.broadcasted_iota(jnp.int32, (rows, block), 1) + base
        before = matmul(count.astype(BF16), onehot(row < col))
        part = route_t[:, span]
        name = lax.broadcasted_iota(jnp.int32, (experts, block), 0)
        line = lax.broadcasted_iota(jnp.int32, (8, block), 0)
        stack = jnp.zeros((8, block), F32)
        for k in range(2):
            mine = part[k : k + 1, :]
            rank = jnp.sum(jnp.where(mine == name, before, 0.0), axis=0, keepdims=True)
            owner = jnp.zeros_like(mine)
            for q in range(1, group):
                owner = owner + (mine >= q * per_dev).astype(jnp.int32)
            place = (mine - owner * per_dev) * group + owner
            slot = place * cap + rank.astype(jnp.int32)
            slot_r[k : k + 1, span] = slot
            stack = jnp.where(line == k, slot.astype(F32), stack)
            stack = jnp.where(line == k + 2, gates_t[k : k + 1, span], stack)
        cols[span, :] = stack.T
        x = tok[span, :].astype(F32)
        centred = x - jnp.mean(x, axis=-1, keepdims=True)
        spread_of = jnp.mean(centred * centred, axis=-1, keepdims=True)
        prep[span, 0:feats] = (x * lax.rsqrt(spread_of + 1e-05) * gain[...]).astype(BF16)
        prep[span, feats : 2 * feats] = dmix[span, :]
        service(i, [
            (min(1, blocks - 1), lambda: ag_own(0, 0)),
            (blocks - 1, lambda: ag_own(2, 0)),
        ])
        return carry

    lax.fori_loop(0, blocks, slots, 0)
    packs = per_dev * tiles

    def pack(i, carry):
        e, jt = i // tiles, lax.rem(i, tiles)
        dest = lax.rem(t + jt, tiles)
        want = lax.broadcasted_iota(jnp.int32, (wide, rows), 0) + (e * group + dest * inner) * cap
        first = slot_r[0:1, :] == want
        second = slot_r[1:2, :] == want
        weight = jnp.where(first, gates_t[0:1, :], jnp.where(second, gates_t[1:2, :], 0.0))
        scale = jnp.sum(weight, axis=1, keepdims=True)
        got = matmul(onehot(jnp.logical_or(first, second)), prep[...])
        xs[e, jt, :, :, 0:feats] = got[:, 0:feats].astype(BF16).reshape(inner, cap, feats)
        xs[e, jt, :, :, feats : 2 * feats] = (
            (scale * got[:, feats : 2 * feats]).astype(BF16).reshape(inner, cap, feats)
        )
        exchange(e, jt, begin, False, False)

        @pl.when(both(jt == tiles - 1, e + 1 < per_dev))
        def _():
            swap_start(e + 1)

        events = []
        for s in range(outer - 1):
            events.append((min(2 * s + 1, packs - 1), functools.partial(ag_event, 0, 0, s)))
            if s == min(1, outer - 2):
                events.append((min(2 * s + 1, packs - 1), lambda: ag_own(1, 0)))
            events.append((min(2 * s + 2, packs - 1), functools.partial(ag_event, 2, 0, s)))
        service(i, events)
        return carry

    lax.fori_loop(0, packs, pack, 0)

    def later(condition, event):
        return lambda: pl.when(condition)(event)

    def inputs(e, i):
        return xr[e, i, :, :, 0:feats].reshape(wide, feats), xr[e, i, :, :, feats : 2 * feats].reshape(wide, feats)

    def expert(e, carry):
        more = e + 1 < per_dev
        before = e >= 1

        def forward(h, events):
            span_h = slice(h * half, (h + 1) * half)
            deeper = blks // 2

            def one(i, carry):
                span = pl.ds(pl.multiple_of(i * wide, wide), wide)
                x, d = inputs(e, i)
                gate_pre = matmul(x, wgu[e, h, 0].reshape(feats, half))
                up_pre = matmul(x, wgu[e, h, 1].reshape(feats, half))
                down = wdn[e, h * deeper : (h + 1) * deeper].reshape(half, feats)
                d_act = matmul(d, down, ((1,), (1,)))
                sigma = jax.nn.sigmoid(gate_pre)
                swish = gate_pre * sigma
                tmp[0, span, span_h] = (swish * up_pre).astype(BF16)
                tmp[1, span, span_h] = (d_act * up_pre * sigma * (1.0 + gate_pre * (1.0 - sigma))).astype(BF16)
                tmp[2, span, span_h] = (d_act * swish).astype(BF16)
                service(i, *events)
                return carry

            lax.fori_loop(0, tiles, one, 0)

        def grads(h):
            x_all = xr[e, :, :, :, 0:feats].reshape(many, feats)
            for g in range(2):
                grad = matmul(x_all, tmp[1 + g, :, h * half : (h + 1) * half], ((0,), (0,)))
                ggu[e, h, g] = grad.astype(BF16).reshape(blks, thin, half)

        width = min(256, hid)

        def downs(i, carry):
            span = pl.ds(pl.multiple_of(i * width, width), width)
            d_all = xr[e, :, :, :, feats : 2 * feats].reshape(many, feats)
            grad = matmul(tmp[0, :, span], d_all, ((0,), (0,)))
            count = width // deep
            gdn[e, pl.ds(i * count, count)] = grad.astype(BF16).reshape(count, deep, feats)
            return carry

        def back(ii, carry):
            jt = lax.rem(ii + 1, tiles)
            i = lax.rem(t + jt, tiles)
            span = pl.ds(pl.multiple_of(i * wide, wide), wide)
            out = matmul(tmp[0, span, :], wdn[e].reshape(hid, feats))
            d_in = jnp.zeros((wide, feats), F32)
            for h in range(2):
                for g in range(2):
                    d_in = d_in + matmul(
                        tmp[1 + g, span, h * half : (h + 1) * half],
                        wgu[e, h, g].reshape(feats, half), ((1,), (1,)),
                    )
            xr[e, i, :, :, 0:feats] = out.astype(BF16).reshape(inner, cap, feats)
            xr[e, i, :, :, feats : 2 * feats] = d_in.astype(BF16).reshape(inner, cap, feats)
            exchange(e, jt, begin, True, False)
            service(ii, *back_events)
            return carry

        def ags(part, e, condition=None):
            events = [functools.partial(ag_event, part, e, s) for s in range(outer - 1)]
            if condition is not None:
                events = [later(condition, event) for event in events]
            return spread(tiles, events)

        everywhere(e, arrive, False, True)

        @pl.when(more)
        def _():
            ag_own(0, e + 1)

        tails = [later(before, event) for event in tail_events(e - 1)]
        forward(0, [ags(1, e), spread(tiles, tails)])
        grads(0)
        rs_start(0, e)

        @pl.when(more)
        def _():
            ag_own(2, e + 1)

        steps = [functools.partial(rs_event, 0, e, step) for step in range(1, outer - 1)]
        forward(1, [
            ags(0, e + 1, more),
            [(min(2 * i + 1, tiles - 1), event) for i, event in enumerate(steps)],
        ])
        grads(1)
        rs_start(1, e)
        lax.fori_loop(0, hid // width, downs, 0)
        rs_start(2, e)
        rs_final(0, e)

        @pl.when(more)
        def _():
            ag_own(1, e + 1)

        steps = []
        for step in range(1, outer - 1):
            steps += [functools.partial(rs_event, 1, e, step), functools.partial(rs_event, 2, e, step)]
        back_events = [ags(2, e + 1, more), spread(tiles, steps), [(tiles - 1, lambda: rs_take(0, e))]]
        lax.fori_loop(0, tiles, back, 0)
        return carry

    def tail_events(e):
        return [
            functools.partial(rs_final, 1, e), functools.partial(rs_final, 2, e),
            functools.partial(rs_take, 1, e), functools.partial(rs_take, 2, e),
        ]

    lax.fori_loop(0, per_dev, expert, 0)

    few = min(256, rows)

    def gather(i, e):
        span = pl.ds(pl.multiple_of(i * few, few), few)
        column = cols[span, :]
        want = lax.broadcasted_iota(jnp.int32, (few, many), 1) + e * many
        first = onehot(column[:, 0:1].astype(jnp.int32) == want)
        second = onehot(column[:, 1:2].astype(jnp.int32) == want)
        value = yr[e].reshape(many, 2 * feats)
        y0 = matmul(first, value[:, 0:feats])
        y1 = matmul(second, value[:, 0:feats])
        dn = matmul(first + second, value[:, feats : 2 * feats])
        return span, column, y0, y1, dn

    def early(e, carry):
        everywhere(e, arrive, True, True)

        def one(i, carry):
            span, column, y0, y1, dn = gather(i, e)
            for k, value in enumerate((y0, y1, dn)):
                lanes = slice(k * feats, (k + 1) * feats)
                old = jnp.where(e == 0, 0.0, acc[span, lanes])
                acc[span, lanes] = old + value
            return carry

        lax.fori_loop(0, rows // few, one, 0)
        return carry

    lax.fori_loop(0, per_dev - 1, early, 0)
    last = per_dev - 1
    ending = tail_events(last)
    ending[0]()
    ending[1]()
    everywhere(last, arrive, True, True)

    def finish(i, carry):
        span, column, y0, y1, dn = gather(i, last)
        if last:
            y0, y1, dn = [
                value + acc[span, k * feats : (k + 1) * feats] for k, value in enumerate((y0, y1, dn))
            ]
        d = dmix[span, :].astype(F32)
        mixed[span, :] = (column[:, 2:3] * y0 + column[:, 3:4] * y1).astype(BF16)
        lane = lax.broadcasted_iota(jnp.int32, (few, 128), 1)
        dots = jnp.where(lane == 0, jnp.sum(d * y0, axis=-1, keepdims=True), 0.0)
        dots = jnp.where(lane == 1, jnp.sum(d * y1, axis=-1, keepdims=True), dots)
        grad_gates[:, span] = dots.T[0:2, :]
        x = tok[span, :].astype(F32)
        centred = x - jnp.mean(x, axis=-1, keepdims=True)
        spread_of = jnp.mean(centred * centred, axis=-1, keepdims=True)
        scale = lax.rsqrt(spread_of + 1e-05)
        u = dn * gain[...]
        pull = jnp.sum(u * x, axis=-1, keepdims=True) * (scale * scale * scale) / feats
        grad_tok[span, :] = (u * scale - pull * centred).astype(BF16)
        return carry

    lax.fori_loop(0, rows // few, finish, 0)
    ending[2]()
    ending[3]()

    def drain(e, carry):
        everywhere(e, leave, False, False)
        everywhere(e, leave, True, False)
        for part in range(3):
            def sent(col):
                for copy in swaps(part, e, col, b, y):
                    copy.wait_send()
                fs_copy(part, e, col, y).wait_send()
            other_columns(sent)
            for way in range(2):
                far = outer - 1 - r if way else r
                for s in range(outer - 1):
                    @pl.when(ag_has(way, s))
                    def _():
                        ag_copy(part, e, way, s, ag_sent_row(way, s)).wait_send()

                    @pl.when(far + s < outer - 1)
                    def _():
                        rs_copy(part, e, way, s).wait_send()
        return carry

    lax.fori_loop(0, per_dev, drain, 0)


def on_device(tiles, blks, tokens, ln_gain, route, gates, w_gate, w_up, w_down, d_mixed):
    rows, feats = tokens.shape
    per_tile, thin, hid = w_gate.shape
    deep = w_down.shape[1]
    experts = per_tile * tiles
    cap = max(2, 3 * rows * route.shape[1] // (2 * experts))
    half = hid // 2
    inner = max(d for d in range(1, math.isqrt(blks) + 1) if blks % d == 0)
    outer = blks // inner
    per_dev = per_tile // inner
    many = tiles * inner * cap
    vmem = pl.BlockSpec(memory_space=pltpu.VMEM)
    hbm = pl.BlockSpec(memory_space=pl.ANY)
    dma = pltpu.SemaphoreType.DMA
    outs = pl.pallas_call(
        functools.partial(kernel, tiles, inner, outer, per_dev, cap),
        out_shape=(
            jax.ShapeDtypeStruct((rows, feats), BF16),
            jax.ShapeDtypeStruct((2, rows), F32),
            jax.ShapeDtypeStruct((rows, feats), BF16),
            jax.ShapeDtypeStruct((per_tile, thin, hid), F32),
            jax.ShapeDtypeStruct((per_tile, thin, hid), F32),
            jax.ShapeDtypeStruct((per_tile, deep, feats), F32),
        ),
        in_specs=[vmem, vmem, vmem, vmem, hbm, hbm, hbm, vmem],
        out_specs=[vmem] * 6,
        scratch_shapes=[
            pltpu.VMEM((per_dev, 2, 2, blks, thin, half), BF16),
            pltpu.VMEM((per_dev, blks, deep, feats), BF16),
            pltpu.VMEM((per_dev, tiles, inner, cap, 2 * feats), BF16),
            pltpu.VMEM((per_dev, tiles, inner, cap, 2 * feats), BF16),
            pltpu.VMEM((per_dev, tiles, inner, cap, 2 * feats), BF16),
            pltpu.VMEM((per_dev, 2, 2, blks, thin, half), BF16),
            pltpu.VMEM((per_dev, blks, deep, feats), BF16),
            pltpu.VMEM((per_dev, 2, 2, outer - 1, 2, inner, thin, half), BF16),
            pltpu.VMEM((per_dev, 2, outer - 1, inner, deep, feats), BF16),
            pltpu.VMEM((per_dev, 2, inner, 2, thin, half), BF16),
            pltpu.VMEM((per_dev, inner, deep, feats), BF16),
            pltpu.VMEM((2, inner, thin, half), F32),
            pltpu.VMEM((inner, deep, feats), F32),
            pltpu.VMEM((rows, 2 * feats), BF16),
            pltpu.VMEM((3, many, hid), BF16),
            pltpu.VMEM((rows if per_dev > 1 else 8, 3 * feats), F32),
            pltpu.VMEM((rows, 8), F32),
            pltpu.VMEM((2, rows), jnp.int32),
            dma((per_dev, 3, 2)),
            dma((per_dev, 3, inner, 2)),
            dma((per_dev, 3, inner, 2)),
            dma((per_dev, 3, 2, outer - 1)),
            dma((per_dev, 3, 2, outer - 1)),
            dma((per_dev, 3, 2, outer - 1)),
            dma((per_dev, 3, 2, outer - 1)),
            dma((per_dev, 3, inner)),
            dma((per_dev, 3, inner)),
            dma((per_dev, tiles, inner)),
            dma((per_dev, tiles, inner)),
            dma((per_dev,)),
            dma((per_dev, tiles, inner)),
            dma((per_dev, tiles, inner)),
            dma((per_dev,)),
        ],
        compiler_params=pltpu.CompilerParams(
            collective_id=0, has_side_effects=True, vmem_limit_bytes=67043328
        ),
    )(tokens, ln_gain.reshape(1, feats), route.T, gates.T, w_gate, w_up, w_down, d_mixed)
    return (outs[0], outs[1].T) + tuple(outs[2:])


def solution(mesh):
    rows_spec = P(("tile", "blk"), None)
    weight_spec = P("tile", "blk", None)
    return jax.shard_map(
        functools.partial(on_device, mesh.shape["tile"], mesh.shape["blk"]),
        mesh=mesh,
        in_specs=(rows_spec, P(), rows_spec, rows_spec) + (weight_spec,) * 3 + (rows_spec,),
        out_specs=(rows_spec,) * 3 + (weight_spec,) * 3,
        check_vma=False,
    )
```

```python
import functools
import math

import jax
import jax.numpy as jnp
from jax import lax
from jax.experimental import pallas as pl
from jax.experimental.pallas import tpu as pltpu
from jax.sharding import PartitionSpec as P

F32 = jnp.float32
BF16 = jnp.bfloat16
MESH = pl.DeviceIdType.MESH


def matmul(left, right, dims=((1,), (0,))):
    return lax.dot_general(left, right, (dims, ((), ())), preferred_element_type=F32)


def onehot(mask):
    return mask.astype(F32).astype(BF16)


def both(*conditions):
    total = conditions[0]
    for condition in conditions[1:]:
        total = jnp.logical_and(total, condition)
    return total


def kernel(
    tiles, inner, outer, per_dev, cap,
    tok, gain, route_t, gates_t, w_gate, w_up, w_down, dmix,
    mixed_h, grad_gates_h, grad_tok_h, out_gate_h, out_up_h, out_dn_h,
    mixed, grad_gates, grad_tok, out_gate, out_up, out_dn, out_sem,
    wgu, wdn, xs, xr, yr, ggu, gdn, rgu, rdn, fgu, fdn, tgu, tdn, prep, tmp, acc, cols, slot_r,
    load_sem, sw_send, sw_recv, ag_send, ag_recv, rs_send, rs_recv, fs_send, fs_recv,
    go_send, go_recv, go_own, back_send, back_recv, back_own,
):
    rows, feats = tok.shape
    hid = w_gate.shape[2]
    blks = inner * outer
    thin, deep = feats // blks, hid // blks
    half = hid // 2
    group = tiles * inner
    wide = inner * cap
    many = tiles * wide
    t = lax.axis_index("tile")
    b = lax.axis_index("blk")
    r = b // inner
    y = lax.rem(b, inner)
    order = (0, 2, 1)

    def device(tile, row, col):
        return dict(device_id=(tile, row * inner + col), device_id_type=MESH)

    def shards(part, name):
        if part == 2:
            return (w_down.at[name],)
        span = slice(part * half, (part + 1) * half)
        return (w_gate.at[name, :, span], w_up.at[name, :, span])

    def places(part, e, blk):
        if part == 2:
            return (wdn.at[e, blk],)
        return (wgu.at[e, part, 0, blk], wgu.at[e, part, 1, blk])

    def loads(part, e):
        return [
            pltpu.make_async_copy(src, dst, load_sem.at[e, part, i])
            for i, (src, dst) in enumerate(zip(shards(part, y * per_dev + e), places(part, e, b)))
        ]

    def swaps(part, e, col, blk, mark):
        return [
            pltpu.make_async_remote_copy(
                src_ref=src, dst_ref=dst, send_sem=sw_send.at[e, part, col, i],
                recv_sem=sw_recv.at[e, part, mark, i], **device(t, r, col),
            )
            for i, (src, dst) in enumerate(zip(shards(part, col * per_dev + e), places(part, e, blk)))
        ]

    def other_columns(action):
        for col in range(inner):
            pl.when(col != y)(functools.partial(action, col))

    def swap_start(e):
        for part in order:
            def go(col):
                for copy in swaps(part, e, col, b, y):
                    copy.start()
            other_columns(go)

    def weight_rows(part, e, row):
        span = pl.ds(row * inner, inner)
        return wdn.at[e, span] if part == 2 else wgu.at[e, part, :, span]

    def ag_copy(part, e, way, s, row):
        ref = weight_rows(part, e, row)
        return pltpu.make_async_remote_copy(
            src_ref=ref, dst_ref=ref, send_sem=ag_send.at[e, part, way, s],
            recv_sem=ag_recv.at[e, part, way, s], **device(t, r - 1 if way else r + 1, y),
        )

    def ag_has(way, s):
        return both(r >= 1, r + s < outer) if way else both(r + 1 < outer, r - s >= 0)

    def ag_sent_row(way, s):
        return r + s if way else r - s

    def ag_own(part, e):
        for copy in loads(part, e):
            copy.wait()

        def land(col):
            for copy in swaps(part, e, col, r * inner + col, col):
                copy.wait_recv()
        other_columns(land)
        for way in range(2):
            @pl.when(ag_has(way, 0))
            def _():
                ag_copy(part, e, way, 0, r).start()

    def ag_event(part, e, s):
        for way in range(2):
            row = r + 1 + s if way else r - 1 - s

            @pl.when(row < outer if way else row >= 0)
            def _():
                ag_copy(part, e, way, s, row).wait_recv()
                if s + 1 < outer - 1:
                    @pl.when(r >= 1 if way else r + 1 < outer)
                    def _():
                        ag_copy(part, e, way, s + 1, row).start()

    def grad_rows(part, e, row):
        span = pl.ds(row * inner, inner)
        return gdn.at[e, span] if part == 2 else ggu.at[e, part, :, span]

    def landed(part, e, way, k):
        return rdn.at[e, way, k] if part == 2 else rgu.at[e, part, way, k]

    def rs_copy(part, e, way, k):
        return pltpu.make_async_remote_copy(
            src_ref=grad_rows(part, e, k if way else outer - 1 - k), dst_ref=landed(part, e, way, k),
            send_sem=rs_send.at[e, part, way, k], recv_sem=rs_recv.at[e, part, way, k],
            **device(t, r - 1 if way else r + 1, y),
        )

    def fs_copy(part, e, col, mark):
        if part == 2:
            src, dst = gdn.at[e, r * inner + col], fdn.at[e, mark]
        else:
            src, dst = ggu.at[e, part, :, r * inner + col], fgu.at[e, part, mark]
        return pltpu.make_async_remote_copy(
            src_ref=src, dst_ref=dst, send_sem=fs_send.at[e, part, col],
            recv_sem=fs_recv.at[e, part, mark], **device(t, r, col),
        )

    def put(part, name, value):
        if part == 2:
            out_dn[name] = value
        else:
            span = slice(part * half, (part + 1) * half)
            out_gate[name, :, span] = value[0]
            out_up[name, :, span] = value[1]

    def rs_start(part, e):
        for way in range(2):
            far = outer - 1 - r if way else r

            @pl.when(far == 0)
            def _():
                for k in range(outer - 1):
                    rs_copy(part, e, way, k).start()

    def rs_event(part, e, step):
        for way in range(2):
            far = outer - 1 - r if way else r

            @pl.when(both(far > 0, far <= step))
            def _():
                k = step - far
                own, new = grad_rows(part, e, k if way else outer - 1 - k), landed(part, e, way, k)
                rs_copy(part, e, way, k).wait_recv()
                own[...] = (own[...].astype(F32) + new[...].astype(F32)).astype(BF16)
                rs_copy(part, e, way, k).start()

    def rs_final(part, e):
        total = tdn if part == 2 else tgu
        total[...] = grad_rows(part, e, r)[...].astype(F32)
        for way in range(2):
            far = outer - 1 - r if way else r

            @pl.when(far > 0)
            def _():
                k = outer - 1 - far
                rs_copy(part, e, way, k).wait_recv()
                total[...] += landed(part, e, way, k)[...].astype(F32)

        for col in range(inner):
            value = total[col] if part == 2 else total[:, col]

            @pl.when(col == y)
            def _():
                put(part, col * per_dev + e, value)

            @pl.when(col != y)
            def _():
                if part == 2:
                    gdn[e, r * inner + col] = value.astype(BF16)
                else:
                    ggu[e, part, :, r * inner + col] = value.astype(BF16)
                fs_copy(part, e, col, y).start()

    def rs_take(part, e):
        def take(col):
            fs_copy(part, e, col, col).wait_recv()
            put(part, col * per_dev + e, (fdn[e, col] if part == 2 else fgu[e, part, col]).astype(F32))
        other_columns(take)

    def exchange(e, jt, action, backward, mark):
        tile = lax.rem(t + jt, tiles)
        from_tile = lax.rem(t - jt + tiles, tiles)
        for col in range(inner):
            if backward:
                src, dst = xr.at[e, tile, col], yr.at[e, t, y]
                landing = yr.at[e, from_tile, col]
                sems = back_send, back_recv, back_own
            else:
                src, dst = xs.at[e, jt, col], xr.at[e, t, y]
                landing = xr.at[e, from_tile, col]
                sems = go_send, go_recv, go_own

            def here():
                return pltpu.make_async_copy(src, dst, sems[2].at[e])

            def there():
                return pltpu.make_async_remote_copy(
                    src_ref=src, dst_ref=landing if mark else dst,
                    send_sem=sems[0].at[e, jt, col], recv_sem=sems[1].at[e, jt, col if mark else y],
                    **device(tile, r, col),
                )

            mine = both(jt == 0, col == y)
            pl.when(mine)(lambda: action(here(), True))
            pl.when(jnp.logical_not(mine))(lambda: action(there(), False))

    def begin(copy, local):
        copy.start()

    def arrive(copy, local):
        if local:
            copy.wait()
        else:
            copy.wait_recv()

    def leave(copy, local):
        if not local:
            copy.wait_send()

    def everywhere(e, action, backward, mark):
        def one(jt, carry):
            exchange(e, jt, action, backward, mark)
            return carry
        lax.fori_loop(0, tiles, one, 0)

    def service(i, *lists):
        for events in lists:
            for place, event in events:
                pl.when(i == place)(event)

    for e in range(per_dev):
        for part in order:
            for copy in loads(part, e):
                copy.start()

    barrier = pltpu.get_barrier_semaphore()
    for jt in range(tiles):
        for col in range(inner):
            @pl.when(jnp.logical_or(jt > 0, col != y))
            def _():
                pl.semaphore_signal(barrier, inc=1, **device(lax.rem(t + jt, tiles), r, col))

    @pl.when(r > 0)
    def _():
        pl.semaphore_signal(barrier, inc=1, **device(t, r - 1, y))

    @pl.when(r + 1 < outer)
    def _():
        pl.semaphore_signal(barrier, inc=1, **device(t, r + 1, y))

    pl.semaphore_wait(
        barrier, group - 1 + jnp.where(r > 0, 1, 0) + jnp.where(r + 1 < outer, 1, 0)
    )
    swap_start(0)

    block = min(256, rows)
    blocks = rows // block

    def slots(i, carry):
        base = pl.multiple_of(i * block, block)
        span = pl.ds(base, block)
        experts = group * per_dev
        names = lax.broadcasted_iota(jnp.int32, (experts, rows), 0)
        count = (route_t[0:1, :] == names).astype(F32) + (route_t[1:2, :] == names).astype(F32)
        row = lax.broadcasted_iota(jnp.int32, (rows, block), 0)
        col = lax.broadcasted_iota(jnp.int32, (rows, block), 1) + base
        before = matmul(count.astype(BF16), onehot(row < col))
        part = route_t[:, span]
        name = lax.broadcasted_iota(jnp.int32, (experts, block), 0)
        line = lax.broadcasted_iota(jnp.int32, (8, block), 0)
        stack = jnp.zeros((8, block), F32)
        for k in range(2):
            mine = part[k : k + 1, :]
            rank = jnp.sum(jnp.where(mine == name, before, 0.0), axis=0, keepdims=True)
            owner = jnp.zeros_like(mine)
            for q in range(1, group):
                owner = owner + (mine >= q * per_dev).astype(jnp.int32)
            place = (mine - owner * per_dev) * group + owner
            slot = place * cap + rank.astype(jnp.int32)
            slot_r[k : k + 1, span] = slot
            stack = jnp.where(line == k, slot.astype(F32), stack)
            stack = jnp.where(line == k + 2, gates_t[k : k + 1, span], stack)
        cols[span, :] = stack.T
        x = tok[span, :].astype(F32)
        centred = x - jnp.mean(x, axis=-1, keepdims=True)
        spread_of = jnp.mean(centred * centred, axis=-1, keepdims=True)
        prep[span, 0:feats] = (x * lax.rsqrt(spread_of + 1e-05) * gain[...]).astype(BF16)
        prep[span, feats : 2 * feats] = dmix[span, :]
        service(i, [(max(0, blocks - 2), lambda: ag_own(0, 0))])
        return carry

    class Steps:
        def __init__(self, events):
            self.events = list(events)

        def run(self, count=1):
            for event in self.events[:count]:
                event()
            self.events = self.events[count:]

        def rest(self):
            self.run(len(self.events))

        def pop(self):
            event = self.events[0]
            self.events = self.events[1:]
            return event

    gathers = {
        (part, e): Steps(functools.partial(ag_event, part, e, s) for s in range(outer - 1))
        for part in range(3) for e in range(per_dev)
    }
    reductions = {
        (part, e): Steps(functools.partial(rs_event, part, e, step) for step in range(1, outer - 1))
        for part in range(3) for e in range(per_dev)
    }

    def pack(e, queue):
        def one(jt, carry):
            dest = lax.rem(t + jt, tiles)
            want = lax.broadcasted_iota(jnp.int32, (wide, rows), 0) + (e * group + dest * inner) * cap
            first = slot_r[0:1, :] == want
            second = slot_r[1:2, :] == want
            weight = jnp.where(first, gates_t[0:1, :], jnp.where(second, gates_t[1:2, :], 0.0))
            scale = jnp.sum(weight, axis=1, keepdims=True)
            got = matmul(onehot(jnp.logical_or(first, second)), prep[...])
            xs[e, jt, :, :, 0:feats] = got[:, 0:feats].astype(BF16).reshape(inner, cap, feats)
            xs[e, jt, :, :, feats : 2 * feats] = (
                (scale * got[:, feats : 2 * feats]).astype(BF16).reshape(inner, cap, feats)
            )
            if e == 0:
                exchange(e, jt, begin, False, False)
            service(jt, [(place, event) for place, event in enumerate(queue[:tiles]) if event])
            return carry

        lax.fori_loop(0, tiles, one, 0)
        for event in queue[tiles:]:
            event()

    def inputs(e, i):
        return xr[e, i, :, :, 0:feats].reshape(wide, feats), xr[e, i, :, :, feats : 2 * feats].reshape(wide, feats)

    def forward(e, h):
        span_h = slice(h * half, (h + 1) * half)
        deeper = blks // 2

        def one(i, carry):
            span = pl.ds(pl.multiple_of(i * wide, wide), wide)
            x, d = inputs(e, i)
            gate_pre = matmul(x, wgu[e, h, 0].reshape(feats, half))
            up_pre = matmul(x, wgu[e, h, 1].reshape(feats, half))
            down = wdn[e, h * deeper : (h + 1) * deeper].reshape(half, feats)
            d_act = matmul(d, down, ((1,), (1,)))
            sigma = jax.nn.sigmoid(gate_pre)
            swish = gate_pre * sigma
            tmp[0, span, span_h] = (swish * up_pre).astype(BF16)
            tmp[1, span, span_h] = (d_act * up_pre * sigma * (1.0 + gate_pre * (1.0 - sigma))).astype(BF16)
            tmp[2, span, span_h] = (d_act * swish).astype(BF16)
            return carry

        lax.fori_loop(0, tiles, one, 0)

    def grads(e, h):
        x_all = xr[e, :, :, :, 0:feats].reshape(many, feats)
        for g in range(2):
            grad = matmul(x_all, tmp[1 + g, :, h * half : (h + 1) * half], ((0,), (0,)))
            ggu[e, h, g] = grad.astype(BF16).reshape(blks, thin, half)
        rs_start(h, e)

    width = min(256, hid)

    def downs(e):
        def one(i, carry):
            span = pl.ds(pl.multiple_of(i * width, width), width)
            d_all = xr[e, :, :, :, feats : 2 * feats].reshape(many, feats)
            grad = matmul(tmp[0, :, span], d_all, ((0,), (0,)))
            count = width // deep
            gdn[e, pl.ds(i * count, count)] = grad.astype(BF16).reshape(count, deep, feats)
            return carry

        lax.fori_loop(0, hid // width, one, 0)
        rs_start(2, e)

    def back(e):
        def one(ii, carry):
            jt = lax.rem(ii + 1, tiles)
            i = lax.rem(t + jt, tiles)
            span = pl.ds(pl.multiple_of(i * wide, wide), wide)
            out = matmul(tmp[0, span, :], wdn[e].reshape(hid, feats))
            d_in = jnp.zeros((wide, feats), F32)
            for h in range(2):
                for g in range(2):
                    d_in = d_in + matmul(
                        tmp[1 + g, span, h * half : (h + 1) * half],
                        wgu[e, h, g].reshape(feats, half), ((1,), (1,)),
                    )
            xr[e, i, :, :, 0:feats] = out.astype(BF16).reshape(inner, cap, feats)
            xr[e, i, :, :, feats : 2 * feats] = d_in.astype(BF16).reshape(inner, cap, feats)
            exchange(e, jt, begin, True, False)
            return carry

        lax.fori_loop(0, tiles, one, 0)

    lax.fori_loop(0, blocks, slots, 0)
    ag_own(2, 0)
    keys = sorted((s + (0.0, 1.2, 0.6)[part], part) for s in range(outer - 1) for part in range(3))
    queue = [None]
    for key, part in keys[:-2]:
        queue.append(gathers[part, 0].pop())
        if len(queue) == 2:
            queue.append(lambda: ag_own(1, 0))
    pack(0, queue[:tiles] if per_dev > 1 else queue)
    for e in range(1, per_dev):
        swap_start(e)
        pack(e, queue[tiles:] if e == 1 else [])

    for e in range(per_dev):
        more, before = e + 1 < per_dev, e > 0
        gathers[0, e].rest()
        if more:
            ag_own(0, e + 1)
        gathers[2, e].rest()
        if more:
            ag_own(2, e + 1)
            gathers[1, e].run()
            ag_own(1, e + 1)
        everywhere(e, arrive, False, True)
        if more:
            everywhere(e + 1, begin, False, False)
        forward(e, 0)
        if not before:
            gathers[1, e].rest()
        if more:
            gathers[0, e + 1].run()
        if before:
            rs_final(1, e - 1)
        grads(e, 0)
        if before:
            reductions[2, e - 1].run()
            gathers[1, e].run()
            reductions[2, e - 1].rest()
            gathers[1, e].rest()
        if more:
            gathers[2, e + 1].run()
            gathers[0, e + 1].run()
        forward(e, 1)
        if more:
            gathers[1, e + 1].run()
            gathers[2, e + 1].run()
            gathers[0, e + 1].rest()
        if before:
            rs_final(2, e - 1)
            rs_take(1, e - 1)
        grads(e, 1)
        reductions[0, e].run()
        downs(e)
        if more:
            gathers[1, e + 1].run()
        back(e)
        if more:
            reductions[0, e].rest()
            gathers[2, e + 1].rest()
            rs_final(0, e)
            reductions[1, e].rest()
            rs_take(0, e)
            if before:
                rs_take(2, e - 1)

    few = min(256, rows)

    def gather(i, e):
        span = pl.ds(pl.multiple_of(i * few, few), few)
        column = cols[span, :]
        want = lax.broadcasted_iota(jnp.int32, (few, many), 1) + e * many
        first = onehot(column[:, 0:1].astype(jnp.int32) == want)
        second = onehot(column[:, 1:2].astype(jnp.int32) == want)
        value = yr[e].reshape(many, 2 * feats)
        y0 = matmul(first, value[:, 0:feats])
        y1 = matmul(second, value[:, 0:feats])
        dn = matmul(first + second, value[:, feats : 2 * feats])
        return span, column, y0, y1, dn

    def early(e):
        def one(i, carry):
            span, column, y0, y1, dn = gather(i, e)
            for k, value in enumerate((y0, y1, dn)):
                lanes = slice(k * feats, (k + 1) * feats)
                acc[span, lanes] = value + acc[span, lanes] if e else value
            return carry

        everywhere(e, arrive, True, True)
        lax.fori_loop(0, rows // few, one, 0)

    last = per_dev - 1
    reductions[0, last].rest()
    rs_final(0, last)
    for e in range(last):
        early(e)
    if last:
        rs_take(2, last - 1)
    reductions[1, last].rest()
    rs_final(1, last)
    reductions[2, last].run()
    everywhere(last, arrive, True, True)

    results = [
        pltpu.make_async_copy(src, dst, out_sem.at[i])
        for i, (src, dst) in enumerate((
            (mixed, mixed_h), (grad_gates, grad_gates_h), (grad_tok, grad_tok_h),
            (out_gate, out_gate_h), (out_up, out_up_h), (out_dn, out_dn_h),
        ))
    ]
    for part in range(2):
        rs_take(part, last)
    for copy in results[3:5]:
        copy.start()
    ending = [reductions[2, last].rest, functools.partial(rs_final, 2, last)]

    def finish(i, carry):
        span, column, y0, y1, dn = gather(i, last)
        if last:
            y0, y1, dn = [
                value + acc[span, k * feats : (k + 1) * feats] for k, value in enumerate((y0, y1, dn))
            ]
        d = dmix[span, :].astype(F32)
        mixed[span, :] = (column[:, 2:3] * y0 + column[:, 3:4] * y1).astype(BF16)
        lane = lax.broadcasted_iota(jnp.int32, (few, 128), 1)
        dots = jnp.where(lane == 0, jnp.sum(d * y0, axis=-1, keepdims=True), 0.0)
        dots = jnp.where(lane == 1, jnp.sum(d * y1, axis=-1, keepdims=True), dots)
        grad_gates[:, span] = dots.T[0:2, :]
        x = tok[span, :].astype(F32)
        centred = x - jnp.mean(x, axis=-1, keepdims=True)
        spread_of = jnp.mean(centred * centred, axis=-1, keepdims=True)
        scale = lax.rsqrt(spread_of + 1e-05)
        u = dn * gain[...]
        pull = jnp.sum(u * x, axis=-1, keepdims=True) * (scale * scale * scale) / feats
        grad_tok[span, :] = (u * scale - pull * centred).astype(BF16)
        service(i, [(min(2 * place, rows // few - 1), event) for place, event in enumerate(ending)])
        return carry

    lax.fori_loop(0, rows // few, finish, 0)
    for copy in results[:3]:
        copy.start()
    rs_take(2, last)
    results[5].start()

    def drain(e, carry):
        everywhere(e, leave, False, False)
        everywhere(e, leave, True, False)
        for part in range(3):
            def sent(col):
                for copy in swaps(part, e, col, b, y):
                    copy.wait_send()
                fs_copy(part, e, col, y).wait_send()
            other_columns(sent)
            for way in range(2):
                far = outer - 1 - r if way else r
                for s in range(outer - 1):
                    @pl.when(ag_has(way, s))
                    def _():
                        ag_copy(part, e, way, s, ag_sent_row(way, s)).wait_send()

                    @pl.when(far + s < outer - 1)
                    def _():
                        rs_copy(part, e, way, s).wait_send()
        return carry

    lax.fori_loop(0, per_dev, drain, 0)
    for copy in results:
        copy.wait()


def hand_over(*refs):
    count = len(refs) // 3
    stage, sems = refs[2 * count : 3 * count], refs[3 * count]
    count_of = range(count)
    into = [pltpu.make_async_copy(refs[i], stage[i], sems.at[0, i]) for i in count_of]
    out = [pltpu.make_async_copy(stage[i], refs[count + i], sems.at[1, i]) for i in count_of]
    for copy in into:
        copy.start()
    for first, second in zip(into, out):
        first.wait()
        second.start()
    for copy in out:
        copy.wait()


def on_device(tiles, blks, tokens, ln_gain, route, gates, w_gate, w_up, w_down, d_mixed):
    rows, feats = tokens.shape
    per_tile, thin, hid = w_gate.shape
    deep = w_down.shape[1]
    experts = per_tile * tiles
    cap = max(2, 3 * rows * route.shape[1] // (2 * experts))
    half = hid // 2
    inner = max(d for d in range(1, math.isqrt(blks) + 1) if blks % d == 0)
    outer = blks // inner
    per_dev = per_tile // inner
    many = tiles * inner * cap
    vmem = pl.BlockSpec(memory_space=pltpu.VMEM)
    hbm = pl.BlockSpec(memory_space=pl.ANY)
    fixed = pl.BlockSpec(memory_space=pltpu.HBM)
    dma = pltpu.SemaphoreType.DMA
    outs = pl.pallas_call(
        functools.partial(kernel, tiles, inner, outer, per_dev, cap),
        out_shape=(
            jax.ShapeDtypeStruct((rows, feats), BF16),
            jax.ShapeDtypeStruct((2, rows), F32),
            jax.ShapeDtypeStruct((rows, feats), BF16),
            jax.ShapeDtypeStruct((per_tile, thin, hid), F32),
            jax.ShapeDtypeStruct((per_tile, thin, hid), F32),
            jax.ShapeDtypeStruct((per_tile, deep, feats), F32),
        ),
        in_specs=[vmem, vmem, vmem, vmem, hbm, hbm, hbm, vmem],
        out_specs=[fixed] * 6,
        scratch_shapes=[
            pltpu.VMEM((rows, feats), BF16),
            pltpu.VMEM((2, rows), F32),
            pltpu.VMEM((rows, feats), BF16),
            pltpu.VMEM((per_tile, thin, hid), F32),
            pltpu.VMEM((per_tile, thin, hid), F32),
            pltpu.VMEM((per_tile, deep, feats), F32),
            dma((6,)),
            pltpu.VMEM((per_dev, 2, 2, blks, thin, half), BF16),
            pltpu.VMEM((per_dev, blks, deep, feats), BF16),
            pltpu.VMEM((per_dev, tiles, inner, cap, 2 * feats), BF16),
            pltpu.VMEM((per_dev, tiles, inner, cap, 2 * feats), BF16),
            pltpu.VMEM((per_dev, tiles, inner, cap, 2 * feats), BF16),
            pltpu.VMEM((per_dev, 2, 2, blks, thin, half), BF16),
            pltpu.VMEM((per_dev, blks, deep, feats), BF16),
            pltpu.VMEM((per_dev, 2, 2, outer - 1, 2, inner, thin, half), BF16),
            pltpu.VMEM((per_dev, 2, outer - 1, inner, deep, feats), BF16),
            pltpu.VMEM((per_dev, 2, inner, 2, thin, half), BF16),
            pltpu.VMEM((per_dev, inner, deep, feats), BF16),
            pltpu.VMEM((2, inner, thin, half), F32),
            pltpu.VMEM((inner, deep, feats), F32),
            pltpu.VMEM((rows, 2 * feats), BF16),
            pltpu.VMEM((3, many, hid), BF16),
            pltpu.VMEM((rows if per_dev > 1 else 8, 3 * feats), F32),
            pltpu.VMEM((rows, 8), F32),
            pltpu.VMEM((2, rows), jnp.int32),
            dma((per_dev, 3, 2)),
            dma((per_dev, 3, inner, 2)),
            dma((per_dev, 3, inner, 2)),
            dma((per_dev, 3, 2, outer - 1)),
            dma((per_dev, 3, 2, outer - 1)),
            dma((per_dev, 3, 2, outer - 1)),
            dma((per_dev, 3, 2, outer - 1)),
            dma((per_dev, 3, inner)),
            dma((per_dev, 3, inner)),
            dma((per_dev, tiles, inner)),
            dma((per_dev, tiles, inner)),
            dma((per_dev,)),
            dma((per_dev, tiles, inner)),
            dma((per_dev, tiles, inner)),
            dma((per_dev,)),
        ],
        compiler_params=pltpu.CompilerParams(
            collective_id=0, has_side_effects=True, vmem_limit_bytes=67043328
        ),
    )(tokens, ln_gain.reshape(1, feats), route.T, gates.T, w_gate, w_up, w_down, d_mixed)
    outs = pl.pallas_call(
        hand_over,
        out_shape=tuple(jax.ShapeDtypeStruct(out.shape, out.dtype) for out in outs),
        in_specs=[fixed] * 6,
        out_specs=[fixed] * 6,
        scratch_shapes=[pltpu.VMEM(out.shape, out.dtype) for out in outs] + [dma((2, 6))],
        compiler_params=pltpu.CompilerParams(vmem_limit_bytes=67043328),
    )(*outs)
    return (outs[0], outs[1].T) + tuple(outs[2:])


def solution(mesh):
    rows_spec = P(("tile", "blk"), None)
    weight_spec = P("tile", "blk", None)
    return jax.shard_map(
        functools.partial(on_device, mesh.shape["tile"], mesh.shape["blk"]),
        mesh=mesh,
        in_specs=(rows_spec, P(), rows_spec, rows_spec) + (weight_spec,) * 3 + (rows_spec,),
        out_specs=(rows_spec,) * 3 + (weight_spec,) * 3,
        check_vma=False,
    )
```

```python
import functools
import math

import jax
import jax.numpy as jnp
from jax import lax
from jax.experimental import pallas as pl
from jax.experimental.pallas import tpu as pltpu
from jax.sharding import PartitionSpec as P

F32 = jnp.float32
BF16 = jnp.bfloat16
MESH = pl.DeviceIdType.MESH


def matmul(left, right, dims=((1,), (0,))):
    return lax.dot_general(left, right, (dims, ((), ())), preferred_element_type=F32)


def onehot(mask):
    return mask.astype(F32).astype(BF16)


def both(*conditions):
    total = conditions[0]
    for condition in conditions[1:]:
        total = jnp.logical_and(total, condition)
    return total


def kernel(
    tiles, inner, outer, per_dev, cap,
    tok, gain, route_t, gates_t, w_gate, w_up, w_down, dmix,
    mixed_h, grad_gates_h, grad_tok_h, out_gate_h, out_up_h, out_dn_h,
    mixed, grad_gates, grad_tok, out_gate, out_up, out_dn, out_sem,
    wgu, wdn, xs, xr, yr, ggu, gdn, rgu, rdn, fgu, fdn, tgu, tdn, prep, tmp, acc, cols, slot_r,
    load_sem, sw_send, sw_recv, ag_send, ag_recv, rs_send, rs_recv, fs_send, fs_recv,
    go_send, go_recv, go_own, back_send, back_recv, back_own,
):
    rows, feats = tok.shape
    hid = w_gate.shape[2]
    blks = inner * outer
    thin, deep = feats // blks, hid // blks
    half = hid // 2
    group = tiles * inner
    wide = inner * cap
    many = tiles * wide
    t = lax.axis_index("tile")
    b = lax.axis_index("blk")
    r = b // inner
    y = lax.rem(b, inner)
    order = (0, 2, 1)

    def device(tile, row, col):
        return dict(device_id=(tile, row * inner + col), device_id_type=MESH)

    def shards(part, name):
        if part == 2:
            return (w_down.at[name],)
        span = slice(part * half, (part + 1) * half)
        return (w_gate.at[name, :, span], w_up.at[name, :, span])

    def places(part, e, blk):
        if part == 2:
            return (wdn.at[e, blk],)
        return (wgu.at[e, part, 0, blk], wgu.at[e, part, 1, blk])

    def loads(part, e):
        return [
            pltpu.make_async_copy(src, dst, load_sem.at[e, part, i])
            for i, (src, dst) in enumerate(zip(shards(part, y * per_dev + e), places(part, e, b)))
        ]

    def swaps(part, e, col, blk, mark):
        return [
            pltpu.make_async_remote_copy(
                src_ref=src, dst_ref=dst, send_sem=sw_send.at[e, part, col, i],
                recv_sem=sw_recv.at[e, part, mark, i], **device(t, r, col),
            )
            for i, (src, dst) in enumerate(zip(shards(part, col * per_dev + e), places(part, e, blk)))
        ]

    def other_columns(action):
        for col in range(inner):
            pl.when(col != y)(functools.partial(action, col))

    def swap_start(e):
        for part in order:
            def go(col):
                for copy in swaps(part, e, col, b, y):
                    copy.start()
            other_columns(go)

    def weight_rows(part, e, row):
        span = pl.ds(row * inner, inner)
        return wdn.at[e, span] if part == 2 else wgu.at[e, part, :, span]

    def ag_copy(part, e, way, s, row):
        ref = weight_rows(part, e, row)
        return pltpu.make_async_remote_copy(
            src_ref=ref, dst_ref=ref, send_sem=ag_send.at[e, part, way, s],
            recv_sem=ag_recv.at[e, part, way, s], **device(t, r - 1 if way else r + 1, y),
        )

    def ag_has(way, s):
        return both(r >= 1, r + s < outer) if way else both(r + 1 < outer, r - s >= 0)

    def ag_sent_row(way, s):
        return r + s if way else r - s

    def ag_own(part, e):
        for copy in loads(part, e):
            copy.wait()

        def land(col):
            for copy in swaps(part, e, col, r * inner + col, col):
                copy.wait_recv()
        other_columns(land)
        for way in range(2):
            @pl.when(ag_has(way, 0))
            def _():
                ag_copy(part, e, way, 0, r).start()

    def ag_event(part, e, s):
        for way in range(2):
            row = r + 1 + s if way else r - 1 - s

            @pl.when(row < outer if way else row >= 0)
            def _():
                ag_copy(part, e, way, s, row).wait_recv()
                if s + 1 < outer - 1:
                    @pl.when(r >= 1 if way else r + 1 < outer)
                    def _():
                        ag_copy(part, e, way, s + 1, row).start()

    def grad_rows(part, e, row):
        span = pl.ds(row * inner, inner)
        return gdn.at[e, span] if part == 2 else ggu.at[e, part, :, span]

    def landed(part, e, way, k):
        return rdn.at[e, way, k] if part == 2 else rgu.at[e, part, way, k]

    def rs_copy(part, e, way, k):
        return pltpu.make_async_remote_copy(
            src_ref=grad_rows(part, e, k if way else outer - 1 - k), dst_ref=landed(part, e, way, k),
            send_sem=rs_send.at[e, part, way, k], recv_sem=rs_recv.at[e, part, way, k],
            **device(t, r - 1 if way else r + 1, y),
        )

    def fs_copy(part, e, col, mark):
        if part == 2:
            src, dst = gdn.at[e, r * inner + col], fdn.at[e, mark]
        else:
            src, dst = ggu.at[e, part, :, r * inner + col], fgu.at[e, part, mark]
        return pltpu.make_async_remote_copy(
            src_ref=src, dst_ref=dst, send_sem=fs_send.at[e, part, col],
            recv_sem=fs_recv.at[e, part, mark], **device(t, r, col),
        )

    def put(part, name, value):
        if part == 2:
            out_dn[name] = value
        else:
            span = slice(part * half, (part + 1) * half)
            out_gate[name, :, span] = value[0]
            out_up[name, :, span] = value[1]

    def rs_start(part, e):
        for way in range(2):
            far = outer - 1 - r if way else r

            @pl.when(far == 0)
            def _():
                for k in range(outer - 1):
                    rs_copy(part, e, way, k).start()

    def rs_event(part, e, step):
        for way in range(2):
            far = outer - 1 - r if way else r

            @pl.when(both(far > 0, far <= step))
            def _():
                k = step - far
                own, new = grad_rows(part, e, k if way else outer - 1 - k), landed(part, e, way, k)
                rs_copy(part, e, way, k).wait_recv()
                own[...] = (own[...].astype(F32) + new[...].astype(F32)).astype(BF16)
                rs_copy(part, e, way, k).start()

    def rs_final(part, e):
        total = tdn if part == 2 else tgu
        total[...] = grad_rows(part, e, r)[...].astype(F32)
        for way in range(2):
            far = outer - 1 - r if way else r

            @pl.when(far > 0)
            def _():
                k = outer - 1 - far
                rs_copy(part, e, way, k).wait_recv()
                total[...] += landed(part, e, way, k)[...].astype(F32)

        for col in range(inner):
            value = total[col] if part == 2 else total[:, col]

            @pl.when(col == y)
            def _():
                put(part, col * per_dev + e, value)

            @pl.when(col != y)
            def _():
                if part == 2:
                    gdn[e, r * inner + col] = value.astype(BF16)
                else:
                    ggu[e, part, :, r * inner + col] = value.astype(BF16)
                fs_copy(part, e, col, y).start()

    def rs_take(part, e):
        def take(col):
            fs_copy(part, e, col, col).wait_recv()
            put(part, col * per_dev + e, (fdn[e, col] if part == 2 else fgu[e, part, col]).astype(F32))
        other_columns(take)

    def exchange(e, jt, action, backward, mark):
        tile = lax.rem(t + jt, tiles)
        from_tile = lax.rem(t - jt + tiles, tiles)
        for col in range(inner):
            if backward:
                src, dst = xr.at[e, tile, col], yr.at[e, t, y]
                landing = yr.at[e, from_tile, col]
                sems = back_send, back_recv, back_own
            else:
                src, dst = xs.at[e, jt, col], xr.at[e, t, y]
                landing = xr.at[e, from_tile, col]
                sems = go_send, go_recv, go_own

            def here():
                return pltpu.make_async_copy(src, dst, sems[2].at[e])

            def there():
                return pltpu.make_async_remote_copy(
                    src_ref=src, dst_ref=landing if mark else dst,
                    send_sem=sems[0].at[e, jt, col], recv_sem=sems[1].at[e, jt, col if mark else y],
                    **device(tile, r, col),
                )

            mine = both(jt == 0, col == y)
            pl.when(mine)(lambda: action(here(), True))
            pl.when(jnp.logical_not(mine))(lambda: action(there(), False))

    def begin(copy, local):
        copy.start()

    def arrive(copy, local):
        if local:
            copy.wait()
        else:
            copy.wait_recv()

    def leave(copy, local):
        if not local:
            copy.wait_send()

    def everywhere(e, action, backward, mark):
        def one(jt, carry):
            exchange(e, jt, action, backward, mark)
            return carry
        lax.fori_loop(0, tiles, one, 0)

    def service(i, *lists):
        for events in lists:
            for place, event in events:
                pl.when(i == place)(event)

    for e in range(per_dev):
        for part in order:
            for copy in loads(part, e):
                copy.start()

    barrier = pltpu.get_barrier_semaphore()
    for jt in range(tiles):
        for col in range(inner):
            @pl.when(jnp.logical_or(jt > 0, col != y))
            def _():
                pl.semaphore_signal(barrier, inc=1, **device(lax.rem(t + jt, tiles), r, col))

    @pl.when(r > 0)
    def _():
        pl.semaphore_signal(barrier, inc=1, **device(t, r - 1, y))

    @pl.when(r + 1 < outer)
    def _():
        pl.semaphore_signal(barrier, inc=1, **device(t, r + 1, y))

    pl.semaphore_wait(
        barrier, group - 1 + jnp.where(r > 0, 1, 0) + jnp.where(r + 1 < outer, 1, 0)
    )
    swap_start(0)

    block = min(256, rows)
    blocks = rows // block

    def slots(i, carry):
        base = pl.multiple_of(i * block, block)
        span = pl.ds(base, block)
        experts = group * per_dev
        names = lax.broadcasted_iota(jnp.int32, (experts, rows), 0)
        count = (route_t[0:1, :] == names).astype(F32) + (route_t[1:2, :] == names).astype(F32)
        row = lax.broadcasted_iota(jnp.int32, (rows, block), 0)
        col = lax.broadcasted_iota(jnp.int32, (rows, block), 1) + base
        before = matmul(count.astype(BF16), onehot(row < col))
        part = route_t[:, span]
        name = lax.broadcasted_iota(jnp.int32, (experts, block), 0)
        line = lax.broadcasted_iota(jnp.int32, (8, block), 0)
        stack = jnp.zeros((8, block), F32)
        for k in range(2):
            mine = part[k : k + 1, :]
            rank = jnp.sum(jnp.where(mine == name, before, 0.0), axis=0, keepdims=True)
            owner = jnp.zeros_like(mine)
            for q in range(1, group):
                owner = owner + (mine >= q * per_dev).astype(jnp.int32)
            place = (mine - owner * per_dev) * group + owner
            slot = place * cap + rank.astype(jnp.int32)
            slot_r[k : k + 1, span] = slot
            stack = jnp.where(line == k, slot.astype(F32), stack)
            stack = jnp.where(line == k + 2, gates_t[k : k + 1, span], stack)
        cols[span, :] = stack.T
        x = tok[span, :].astype(F32)
        centred = x - jnp.mean(x, axis=-1, keepdims=True)
        spread_of = jnp.mean(centred * centred, axis=-1, keepdims=True)
        prep[span, 0:feats] = (x * lax.rsqrt(spread_of + 1e-05) * gain[...]).astype(BF16)
        prep[span, feats : 2 * feats] = dmix[span, :]
        service(i, [(max(0, blocks - 2), lambda: ag_own(0, 0))])
        return carry

    class Steps:
        def __init__(self, events):
            self.events = list(events)

        def run(self, count=1):
            for event in self.events[:count]:
                event()
            self.events = self.events[count:]

        def rest(self):
            self.run(len(self.events))

        def pop(self):
            event = self.events[0]
            self.events = self.events[1:]
            return event

    gathers = {
        (part, e): Steps(functools.partial(ag_event, part, e, s) for s in range(outer - 1))
        for part in range(3) for e in range(per_dev)
    }
    reductions = {
        (part, e): Steps(functools.partial(rs_event, part, e, step) for step in range(1, outer - 1))
        for part in range(3) for e in range(per_dev)
    }

    def pack(e, queue):
        def one(jt, carry):
            dest = lax.rem(t + jt, tiles)
            want = lax.broadcasted_iota(jnp.int32, (wide, rows), 0) + (e * group + dest * inner) * cap
            first = slot_r[0:1, :] == want
            second = slot_r[1:2, :] == want
            weight = jnp.where(first, gates_t[0:1, :], jnp.where(second, gates_t[1:2, :], 0.0))
            scale = jnp.sum(weight, axis=1, keepdims=True)
            got = matmul(onehot(jnp.logical_or(first, second)), prep[...])
            xs[e, jt, :, :, 0:feats] = got[:, 0:feats].astype(BF16).reshape(inner, cap, feats)
            xs[e, jt, :, :, feats : 2 * feats] = (
                (scale * got[:, feats : 2 * feats]).astype(BF16).reshape(inner, cap, feats)
            )
            if e == 0:
                exchange(e, jt, begin, False, False)
            service(jt, [(place, event) for place, event in enumerate(queue[:tiles]) if event])
            return carry

        lax.fori_loop(0, tiles, one, 0)
        for event in queue[tiles:]:
            event()

    def inputs(e, i):
        return xr[e, i, :, :, 0:feats].reshape(wide, feats), xr[e, i, :, :, feats : 2 * feats].reshape(wide, feats)

    def forward(e, h):
        span_h = slice(h * half, (h + 1) * half)
        deeper = blks // 2

        def one(i, carry):
            span = pl.ds(pl.multiple_of(i * wide, wide), wide)
            x, d = inputs(e, i)
            gate_pre = matmul(x, wgu[e, h, 0].reshape(feats, half))
            up_pre = matmul(x, wgu[e, h, 1].reshape(feats, half))
            down = wdn[e, h * deeper : (h + 1) * deeper].reshape(half, feats)
            d_act = matmul(d, down, ((1,), (1,)))
            sigma = jax.nn.sigmoid(gate_pre)
            swish = gate_pre * sigma
            tmp[0, span, span_h] = (swish * up_pre).astype(BF16)
            tmp[1, span, span_h] = (d_act * up_pre * sigma * (1.0 + gate_pre * (1.0 - sigma))).astype(BF16)
            tmp[2, span, span_h] = (d_act * swish).astype(BF16)
            return carry

        lax.fori_loop(0, tiles, one, 0)

    def grads(e, h):
        x_all = xr[e, :, :, :, 0:feats].reshape(many, feats)
        for g in range(2):
            grad = matmul(x_all, tmp[1 + g, :, h * half : (h + 1) * half], ((0,), (0,)))
            ggu[e, h, g] = grad.astype(BF16).reshape(blks, thin, half)
        rs_start(h, e)

    width = min(256, hid)

    def downs(e):
        def one(i, carry):
            span = pl.ds(pl.multiple_of(i * width, width), width)
            d_all = xr[e, :, :, :, feats : 2 * feats].reshape(many, feats)
            grad = matmul(tmp[0, :, span], d_all, ((0,), (0,)))
            count = width // deep
            gdn[e, pl.ds(i * count, count)] = grad.astype(BF16).reshape(count, deep, feats)
            return carry

        lax.fori_loop(0, hid // width, one, 0)
        rs_start(2, e)

    def back(e):
        def one(ii, carry):
            jt = lax.rem(ii + 1, tiles)
            i = lax.rem(t + jt, tiles)
            span = pl.ds(pl.multiple_of(i * wide, wide), wide)
            out = matmul(tmp[0, span, :], wdn[e].reshape(hid, feats))
            d_in = jnp.zeros((wide, feats), F32)
            for h in range(2):
                for g in range(2):
                    d_in = d_in + matmul(
                        tmp[1 + g, span, h * half : (h + 1) * half],
                        wgu[e, h, g].reshape(feats, half), ((1,), (1,)),
                    )
            xr[e, i, :, :, 0:feats] = out.astype(BF16).reshape(inner, cap, feats)
            xr[e, i, :, :, feats : 2 * feats] = d_in.astype(BF16).reshape(inner, cap, feats)
            exchange(e, jt, begin, True, False)
            return carry

        lax.fori_loop(0, tiles, one, 0)

    lax.fori_loop(0, blocks, slots, 0)
    ag_own(2, 0)
    keys = sorted((s + (0.0, 1.2, 0.6)[part], part) for s in range(outer - 1) for part in range(3))
    queue = [None]
    for key, part in keys[:-2]:
        queue.append(gathers[part, 0].pop())
        if len(queue) == 2:
            queue.append(lambda: ag_own(1, 0))
    pack(0, queue[:tiles] if per_dev > 1 else queue)
    for e in range(1, per_dev):
        swap_start(e)
        pack(e, queue[tiles:] if e == 1 else [])

    for e in range(per_dev):
        more, before = e + 1 < per_dev, e > 0
        gathers[0, e].rest()
        if more:
            ag_own(0, e + 1)
        gathers[2, e].rest()
        if more:
            ag_own(2, e + 1)
            gathers[1, e].run()
            ag_own(1, e + 1)
        everywhere(e, arrive, False, True)
        if more:
            everywhere(e + 1, begin, False, False)
        forward(e, 0)
        if not before:
            gathers[1, e].rest()
        if more:
            gathers[0, e + 1].run()
        if before:
            rs_final(1, e - 1)
        grads(e, 0)
        if before:
            reductions[2, e - 1].run()
            gathers[1, e].run()
            reductions[2, e - 1].rest()
            gathers[1, e].rest()
        if more:
            gathers[2, e + 1].run()
            gathers[0, e + 1].run()
        forward(e, 1)
        if more:
            gathers[1, e + 1].run()
            gathers[2, e + 1].run()
            gathers[0, e + 1].rest()
        if before:
            rs_final(2, e - 1)
        grads(e, 1)
        reductions[0, e].run()
        downs(e)
        if more:
            gathers[1, e + 1].run()
        back(e)
        if more:
            reductions[0, e].rest()
            gathers[2, e + 1].rest()
            rs_final(0, e)
            reductions[1, e].rest()

    few = min(256, rows)

    def gather(i, e):
        span = pl.ds(pl.multiple_of(i * few, few), few)
        column = cols[span, :]
        want = lax.broadcasted_iota(jnp.int32, (few, many), 1) + e * many
        first = onehot(column[:, 0:1].astype(jnp.int32) == want)
        second = onehot(column[:, 1:2].astype(jnp.int32) == want)
        value = yr[e].reshape(many, 2 * feats)
        y0 = matmul(first, value[:, 0:feats])
        y1 = matmul(second, value[:, 0:feats])
        dn = matmul(first + second, value[:, feats : 2 * feats])
        return span, column, y0, y1, dn

    def early(e):
        def one(i, carry):
            span, column, y0, y1, dn = gather(i, e)
            for k, value in enumerate((y0, y1, dn)):
                lanes = slice(k * feats, (k + 1) * feats)
                acc[span, lanes] = value + acc[span, lanes] if e else value
            return carry

        everywhere(e, arrive, True, True)
        lax.fori_loop(0, rows // few, one, 0)

    last = per_dev - 1
    reductions[0, last].rest()
    rs_final(0, last)
    for e in range(last):
        early(e)
    reductions[1, last].rest()
    rs_final(1, last)
    reductions[2, last].run()
    everywhere(last, arrive, True, True)

    results = [
        pltpu.make_async_copy(src, dst, out_sem.at[i])
        for i, (src, dst) in enumerate((
            (mixed, mixed_h), (grad_gates, grad_gates_h), (grad_tok, grad_tok_h),
            (out_gate, out_gate_h), (out_up, out_up_h), (out_dn, out_dn_h),
        ))
    ]
    for e in range(last):
        for part in range(3):
            rs_take(part, e)
    ending = [reductions[2, last].rest, functools.partial(rs_final, 2, last)]

    def finish(i, carry):
        span, column, y0, y1, dn = gather(i, last)
        if last:
            y0, y1, dn = [
                value + acc[span, k * feats : (k + 1) * feats] for k, value in enumerate((y0, y1, dn))
            ]
        d = dmix[span, :].astype(F32)
        mixed[span, :] = (column[:, 2:3] * y0 + column[:, 3:4] * y1).astype(BF16)
        lane = lax.broadcasted_iota(jnp.int32, (few, 128), 1)
        dots = jnp.where(lane == 0, jnp.sum(d * y0, axis=-1, keepdims=True), 0.0)
        dots = jnp.where(lane == 1, jnp.sum(d * y1, axis=-1, keepdims=True), dots)
        grad_gates[:, span] = dots.T[0:2, :]
        x = tok[span, :].astype(F32)
        centred = x - jnp.mean(x, axis=-1, keepdims=True)
        spread_of = jnp.mean(centred * centred, axis=-1, keepdims=True)
        scale = lax.rsqrt(spread_of + 1e-05)
        u = dn * gain[...]
        pull = jnp.sum(u * x, axis=-1, keepdims=True) * (scale * scale * scale) / feats
        grad_tok[span, :] = (u * scale - pull * centred).astype(BF16)
        service(i, [(min(2 * place, rows // few - 1), event) for place, event in enumerate(ending)])
        return carry

    lax.fori_loop(0, rows // few, finish, 0)
    for copy in results[:3]:
        copy.start()
    for part in range(3):
        rs_take(part, last)
    for copy in results[3:]:
        copy.start()

    def drain(e, carry):
        everywhere(e, leave, False, False)
        everywhere(e, leave, True, False)
        for part in range(3):
            def sent(col):
                for copy in swaps(part, e, col, b, y):
                    copy.wait_send()
                fs_copy(part, e, col, y).wait_send()
            other_columns(sent)
            for way in range(2):
                far = outer - 1 - r if way else r
                for s in range(outer - 1):
                    @pl.when(ag_has(way, s))
                    def _():
                        ag_copy(part, e, way, s, ag_sent_row(way, s)).wait_send()

                    @pl.when(far + s < outer - 1)
                    def _():
                        rs_copy(part, e, way, s).wait_send()
        return carry

    lax.fori_loop(0, per_dev, drain, 0)
    for copy in results:
        copy.wait()


def hand_over(*refs):
    count = len(refs) // 3
    stage, sems = refs[2 * count : 3 * count], refs[3 * count]
    count_of = range(count)
    into = [pltpu.make_async_copy(refs[i], stage[i], sems.at[0, i]) for i in count_of]
    out = [pltpu.make_async_copy(stage[i], refs[count + i], sems.at[1, i]) for i in count_of]
    for copy in into:
        copy.start()
    for first, second in zip(into, out):
        first.wait()
        second.start()
    for copy in out:
        copy.wait()


def on_device(tiles, blks, tokens, ln_gain, route, gates, w_gate, w_up, w_down, d_mixed):
    rows, feats = tokens.shape
    per_tile, thin, hid = w_gate.shape
    deep = w_down.shape[1]
    experts = per_tile * tiles
    cap = max(2, 3 * rows * route.shape[1] // (2 * experts))
    half = hid // 2
    inner = max(d for d in range(1, math.isqrt(blks) + 1) if blks % d == 0)
    outer = blks // inner
    per_dev = per_tile // inner
    many = tiles * inner * cap
    vmem = pl.BlockSpec(memory_space=pltpu.VMEM)
    hbm = pl.BlockSpec(memory_space=pl.ANY)
    fixed = pl.BlockSpec(memory_space=pltpu.HBM)
    dma = pltpu.SemaphoreType.DMA
    outs = pl.pallas_call(
        functools.partial(kernel, tiles, inner, outer, per_dev, cap),
        out_shape=(
            jax.ShapeDtypeStruct((rows, feats), BF16),
            jax.ShapeDtypeStruct((2, rows), F32),
            jax.ShapeDtypeStruct((rows, feats), BF16),
            jax.ShapeDtypeStruct((per_tile, thin, hid), F32),
            jax.ShapeDtypeStruct((per_tile, thin, hid), F32),
            jax.ShapeDtypeStruct((per_tile, deep, feats), F32),
        ),
        in_specs=[vmem, vmem, vmem, vmem, hbm, hbm, hbm, vmem],
        out_specs=[fixed] * 6,
        scratch_shapes=[
            pltpu.VMEM((rows, feats), BF16),
            pltpu.VMEM((2, rows), F32),
            pltpu.VMEM((rows, feats), BF16),
            pltpu.VMEM((per_tile, thin, hid), F32),
            pltpu.VMEM((per_tile, thin, hid), F32),
            pltpu.VMEM((per_tile, deep, feats), F32),
            dma((6,)),
            pltpu.VMEM((per_dev, 2, 2, blks, thin, half), BF16),
            pltpu.VMEM((per_dev, blks, deep, feats), BF16),
            pltpu.VMEM((per_dev, tiles, inner, cap, 2 * feats), BF16),
            pltpu.VMEM((per_dev, tiles, inner, cap, 2 * feats), BF16),
            pltpu.VMEM((per_dev, tiles, inner, cap, 2 * feats), BF16),
            pltpu.VMEM((per_dev, 2, 2, blks, thin, half), BF16),
            pltpu.VMEM((per_dev, blks, deep, feats), BF16),
            pltpu.VMEM((per_dev, 2, 2, outer - 1, 2, inner, thin, half), BF16),
            pltpu.VMEM((per_dev, 2, outer - 1, inner, deep, feats), BF16),
            pltpu.VMEM((per_dev, 2, inner, 2, thin, half), BF16),
            pltpu.VMEM((per_dev, inner, deep, feats), BF16),
            pltpu.VMEM((2, inner, thin, half), F32),
            pltpu.VMEM((inner, deep, feats), F32),
            pltpu.VMEM((rows, 2 * feats), BF16),
            pltpu.VMEM((3, many, hid), BF16),
            pltpu.VMEM((rows if per_dev > 1 else 8, 3 * feats), F32),
            pltpu.VMEM((rows, 8), F32),
            pltpu.VMEM((2, rows), jnp.int32),
            dma((per_dev, 3, 2)),
            dma((per_dev, 3, inner, 2)),
            dma((per_dev, 3, inner, 2)),
            dma((per_dev, 3, 2, outer - 1)),
            dma((per_dev, 3, 2, outer - 1)),
            dma((per_dev, 3, 2, outer - 1)),
            dma((per_dev, 3, 2, outer - 1)),
            dma((per_dev, 3, inner)),
            dma((per_dev, 3, inner)),
            dma((per_dev, tiles, inner)),
            dma((per_dev, tiles, inner)),
            dma((per_dev,)),
            dma((per_dev, tiles, inner)),
            dma((per_dev, tiles, inner)),
            dma((per_dev,)),
        ],
        compiler_params=pltpu.CompilerParams(
            collective_id=0, has_side_effects=True, vmem_limit_bytes=67043328
        ),
    )(tokens, ln_gain.reshape(1, feats), route.T, gates.T, w_gate, w_up, w_down, d_mixed)
    outs = pl.pallas_call(
        hand_over,
        out_shape=tuple(jax.ShapeDtypeStruct(out.shape, out.dtype) for out in outs),
        in_specs=[fixed] * 6,
        out_specs=[fixed] * 6,
        scratch_shapes=[pltpu.VMEM(out.shape, out.dtype) for out in outs] + [dma((2, 6))],
        compiler_params=pltpu.CompilerParams(vmem_limit_bytes=67043328),
    )(*outs)
    return (outs[0], outs[1].T) + tuple(outs[2:])


def solution(mesh):
    rows_spec = P(("tile", "blk"), None)
    weight_spec = P("tile", "blk", None)
    return jax.shard_map(
        functools.partial(on_device, mesh.shape["tile"], mesh.shape["blk"]),
        mesh=mesh,
        in_specs=(rows_spec, P(), rows_spec, rows_spec) + (weight_spec,) * 3 + (rows_spec,),
        out_specs=(rows_spec,) * 3 + (weight_spec,) * 3,
        check_vma=False,
    )
```
